32 devices in a mesh: groups: 2 (over y), chan: 4 (over z), win: 2 (over x), sub: 2 (over core).
Axes of the slice: x: 2, y: 2, z: 4, core: 2. Of those that a mesh axis runs over, the one named last changes fastest.
Arguments:
- traces: bfloat16 [4, 2560, 1024], P(('groups', 'win'), 'chan'), parts along dimension 0, may hold values from -240 to 240, as said below
- channel_mask: int32 [5120], P(('groups', 'chan')), parts along dimension 0, may hold values 0 or 1
- smooth_width: int32 [512], replicated, may hold values from 1 to 16, as said below
- source_phase: int32 [8], P('groups'), parts along dimension 0, may hold values from 0 to 7
- pair_list: int32 [8, 5], P('groups'), parts along dimension 0, may hold values 0 or 1
Outputs:
- receiver_stack: float32 [8, 5, 101, 5120], P(('win', 'sub'), None, None, ('groups', 'chan')), parts along dimension 3
- source_stack: float32 [64, 5, 101, 640], P(('groups', 'chan', 'win', 'sub')), parts along dimension 0
The draws below stay inside these ranges and needn't reach their ends.
There are 2 independent parts, one for each index of `groups`. The reference program is written for one: setup_inputs(seed, part) draws one part's arguments, and reference() takes and returns one part's arrays. A program takes and returns all parts, laid end to end along the dimension named above; an argument that names none is the same for every part. Nothing has to cross between parts.
Inputs may be any that keep to these rules, and one draw needn't show every extreme that they name: `traces`: float samples; each channel and each window has a scale of its own. `smooth_width`: every value from 1 to 16 may occur; 16 occurs in every draw.
All inputs are finite; a program needn't handle non-finite values. No bound on the sum of `channel_mask` on one device may be relied on, other than what follows from the above.
Results may differ from the reference program's by a relative error of at most 0.0052.
Values may be sent and summed in bfloat16 or wider, within the bound.
A program may use at most 192 MiB of HBM per device.

```python
import math
import jax
import jax.numpy as jnp
from jax import lax

NB = 512
MAXLAG = 50
STRIDE = 8
SMAX = 16
REACH = 2
CB = 640
VS = 8
LSAMP = 1024
LAGS = 101
OFFS = 5
NBLK = 4
NCH = 2560
NSRC = 32
WINDOWS = 2


def draw_traces(key, part):
    k_noise, k_chan, k_win = jax.random.split(key, 3)
    chan_scale = jnp.exp(jax.random.uniform(k_chan, (NCH,), jnp.float32, 0.0, math.log(10.0)))
    win_scale = jnp.exp(jax.random.uniform(k_win, (WINDOWS,), jnp.float32, 0.0, math.log(4.0)))
    noise_draw = jnp.clip(jax.random.normal(k_noise, (WINDOWS, NCH, LSAMP), jnp.float32), -6.0, 6.0)
    return (noise_draw * chan_scale[None, :, None] * win_scale[:, None, None]).astype(jnp.bfloat16)


def draw_smooth_width(key, part):
    k_vals, k_pos = jax.random.split(jax.random.fold_in(key, 17))
    widths = jax.random.randint(k_vals, (NB,), 1, SMAX + 1)
    spot_ids = jax.random.randint(k_pos, (2,), 0, NB)
    bin_ids = jnp.arange(NB)
    widths = jnp.where(bin_ids == spot_ids[0], SMAX, widths)
    widths = jnp.where((bin_ids == spot_ids[1]) & (bin_ids != spot_ids[0]), 1, widths)
    return widths.astype(jnp.int32)


def place_ends(entries, stream_key, least, largest):
    place = [jax.random.randint(jax.random.fold_in(stream_key, axis), (), 0, length) for axis, length in enumerate(entries.shape)]
    main_axis = entries.shape.index(max(entries.shape))
    neighbour = place[:main_axis] + [(place[main_axis] + 1) % entries.shape[main_axis]] + place[main_axis + 1:]
    return entries.at[tuple(place)].set(least).at[tuple(neighbour)].set(largest)


def setup_inputs(seed: int = 0, part: int = 0) -> dict:
    keys = jax.random.split(jax.random.key(seed), 6)
    own_keys = jax.random.split(jax.random.fold_in(keys[5], part), 6)
    return {
        "traces": draw_traces(jax.random.fold_in(jax.random.fold_in(keys[5], part), 71), part),
        "channel_mask": place_ends((jax.random.randint(own_keys[1], (NCH,), 0, 8) < 7).astype(jnp.int32), jax.random.fold_in(own_keys[1], 1), 0, 1),
        "smooth_width": draw_smooth_width(jax.random.fold_in(keys[5], 71), part),
        "source_phase": place_ends(jax.random.randint(own_keys[3], (NBLK,), 0, STRIDE), jax.random.fold_in(own_keys[3], 1), 0, STRIDE - 1).astype(jnp.int32),
        "pair_list": place_ends((jax.random.randint(own_keys[4], (NBLK, OFFS), 0, 4) < 3).astype(jnp.int32), jax.random.fold_in(own_keys[4], 1), 0, 1),
    }


FLOOR = 0.25

def dft_tables(samples, bin_ids):
    sample_ids = jnp.arange(samples, dtype=jnp.int32)
    phases = sample_ids[:, None] * bin_ids[None, :] % samples
    angles = phases.astype(jnp.float32) * (2.0 * math.pi / samples)
    return jnp.concatenate([jnp.cos(angles), -jnp.sin(angles)], axis=1)

def lag_tables(samples, bin_ids, maxlag):
    lag_ids = jnp.arange(2 * maxlag + 1, dtype=jnp.int32) - maxlag
    phases = lag_ids[:, None] * bin_ids[None, :] % samples
    angles = phases.astype(jnp.float32) * (2.0 * math.pi / samples)
    return jnp.stack([jnp.cos(angles), -jnp.sin(angles)], axis=1)

def smoothing_weights(row_ids, bin_ids, widths, bin_total):
    nearby = jnp.abs(row_ids[:, None] - bin_ids[None, :]) <= widths[None, :]
    inside = (row_ids >= 0) & (row_ids < bin_total)
    return jnp.where(nearby & inside[:, None], 1.0, 0.0).astype(jnp.float32)

def cross_lags(sources, spectra, lag_tab):
    turned = jnp.stack([sources[:, 1], -sources[:, 0]], axis=1)
    stacked_pair = jnp.stack([sources, turned], axis=0)
    cross_spec = jnp.einsum('pwqvk,wqkc->pkvc', stacked_pair, spectra, precision=lax.Precision.HIGHEST)
    return jnp.einsum('tpk,pkvc->vtc', lag_tab, cross_spec, precision=lax.Precision.HIGHEST)

def reference(traces, channel_mask, smooth_width, source_phase, pair_list):
    bin_ids = jnp.arange(NB, dtype=jnp.int32)
    tables = dft_tables(LSAMP, bin_ids).astype(jnp.bfloat16)
    tables = lax.optimization_barrier(tables).astype(jnp.float32)
    spectrum = jnp.einsum('wcn,nk->wkc', traces.astype(jnp.float32), tables, precision=lax.Precision.HIGHEST) * LSAMP ** (-0.5)
    spectrum = spectrum * channel_mask.astype(jnp.float32)[None, None, :]
    spectrum = spectrum.reshape(WINDOWS, 2, NB, NCH)
    amplitude = jnp.sqrt(spectrum[:, 0] ** 2 + spectrum[:, 1] ** 2)
    weights = smoothing_weights(bin_ids, bin_ids, smooth_width, NB)
    smoothed = jnp.einsum('wjc,jk->wkc', amplitude, weights, precision=lax.Precision.HIGHEST) / lax.optimization_barrier(jnp.sum(weights, axis=0))[None, :, None]
    whitened = (spectrum / jnp.maximum(smoothed, FLOOR)[:, None]).astype(jnp.bfloat16)
    white_full = lax.optimization_barrier(whitened).astype(jnp.float32)
    grouped = white_full.reshape(WINDOWS, 2, NB, NBLK, CB // STRIDE, STRIDE)[:, :, :, :, :VS]
    picker = jnp.where(jnp.arange(STRIDE, dtype=jnp.int32)[None, :] == source_phase[:, None], 1.0, 0.0).astype(jnp.float32)
    sources = jnp.einsum('wqkbvs,bs->bwqvk', grouped, picker, precision=lax.Precision.HIGHEST)
    receivers = jnp.transpose(white_full.reshape(WINDOWS, 2, NB, NBLK, CB), (3, 0, 1, 2, 4))
    lag_tab = lag_tables(LSAMP, bin_ids, MAXLAG)
    factor = (NB * WINDOWS) ** (-0.5)
    stacks = []
    for offset in range(OFFS):
        moved_by = offset - REACH
        moved = jnp.roll(sources, moved_by, axis=0)
        paired = jnp.roll(pair_list[:, offset], moved_by).astype(jnp.float32)

        def one_block(block_items):
            return cross_lags(block_items[0], block_items[1], lag_tab) * block_items[2]
        lags_block = lax.map(one_block, (moved, receivers, paired))
        stacks.append(lags_block * factor)
    stacked = jnp.stack(stacks, axis=0)
    receiver_stack = jnp.transpose(stacked, (2, 0, 3, 1, 4)).reshape(VS, OFFS, LAGS, NCH)
    turned_back = []
    for offset in range(OFFS):
        moved_by = offset - REACH
        turned_back.append(jnp.flip(jnp.roll(stacked[offset], -moved_by, axis=0), axis=2))
    source_stack = jnp.transpose(jnp.stack(turned_back, axis=0), (1, 2, 0, 3, 4)).reshape(NSRC, OFFS, LAGS, CB)
    return (receiver_stack, source_stack)
```

```python
import math

import jax
import jax.numpy as jnp
import numpy as np
from jax import lax
from jax.sharding import PartitionSpec as P

NB = 512
MAXLAG = 50
LAGS = 2 * MAXLAG + 1
ROWS = 112
STRIDE = 8
REACH = 2
VS = 8
OFFS = 5
FLOOR = 0.25


def from_behind(block, axis, distance):
    devices = range(lax.axis_size(axis))
    if distance % len(devices) == 0:
        return block
    route = [((i - distance) % len(devices), i) for i in devices]
    return lax.ppermute(block, axis, route)


def dft_rows(samples):
    phases = np.arange(NB)[:, None] * np.arange(samples)[None, :] % samples
    angles = phases * (2.0 * math.pi / samples)
    return jnp.asarray(np.concatenate([np.cos(angles), -np.sin(angles)], axis=0), jnp.bfloat16)


def lag_rows(samples):
    lags = np.zeros((2, ROWS), np.int64)
    lags[0, :LAGS] = np.arange(LAGS) - MAXLAG
    lags[1, :LAGS] = MAXLAG - np.arange(LAGS)
    phases = lags[:, :, None] * np.arange(NB) % samples
    angles = phases * (2.0 * math.pi / samples)
    return np.cos(angles).astype(np.float32), np.sin(angles).astype(np.float32)


def on_device(traces, channel_mask, smooth_width, source_phase, pair_list):
    windows, channels, samples = traces.shape
    sub_count = lax.axis_size("sub")
    win_count = lax.axis_size("win")
    blocks = lax.axis_size("chan")
    block_at = lax.axis_index("chan")
    total_windows = windows * win_count
    mine = VS // (win_count * sub_count)
    place = lax.axis_index("win") * sub_count + lax.axis_index("sub")
    scale = channel_mask.astype(jnp.float32) * samples ** (-0.5)

    spectrum = jnp.einsum(
        "mn,wcn->wmc", dft_rows(samples), traces, preferred_element_type=jnp.float32
    ) * scale
    spectrum = spectrum.reshape(windows, 2, NB, channels)
    amplitude = jnp.sqrt(spectrum[:, 0] ** 2 + spectrum[:, 1] ** 2)
    bins = jnp.arange(NB, dtype=jnp.int32)
    near = jnp.abs(bins[:, None] - bins[None, :]) <= smooth_width[:, None]
    weights = near.astype(jnp.bfloat16)
    count = jnp.sum(near.astype(jnp.float32), axis=1)
    high = amplitude.astype(jnp.bfloat16)
    low = (amplitude - high.astype(jnp.float32)).astype(jnp.bfloat16)
    total = jnp.einsum("kj,wjc->wkc", weights, high, preferred_element_type=jnp.float32)
    total = total + jnp.einsum("kj,wjc->wkc", weights, low, preferred_element_type=jnp.float32)
    smoothed = total / count[None, :, None]
    whitened = (spectrum / jnp.maximum(smoothed, FLOOR)[:, None]).astype(jnp.bfloat16)

    phase = source_phase[block_at]
    wanted = phase + STRIDE * jnp.arange(VS, dtype=jnp.int32)
    picker = (jnp.arange(channels, dtype=jnp.int32)[None, :] == wanted[:, None]).astype(jnp.bfloat16)
    own = jnp.einsum(
        "vc,wqkc->vwqk", picker, whitened, preferred_element_type=jnp.float32
    ).astype(jnp.bfloat16)
    own_all = jnp.concatenate([from_behind(own, "win", d) for d in range(win_count)], axis=1)
    own_mine = lax.dynamic_slice_in_dim(own_all, place * mine, mine, axis=0)
    spectra = jnp.concatenate([from_behind(whitened, "win", d) for d in range(win_count)], axis=0)
    spectra = spectra.reshape(total_windows * 2 * NB, channels)

    cosines, sines = lag_rows(samples)
    factor = (NB * total_windows) ** (-0.5)
    cosines = jnp.asarray(cosines * np.float32(factor))[None, :, :, None, :]
    sines = jnp.asarray(sines * np.float32(factor))[None, :, :, None, :]
    pieces = {}
    for offset in range(OFFS):
        key = (offset - REACH) % blocks
        if key in pieces:
            continue
        near_sources = from_behind(own_mine, "chan", key).astype(jnp.float32)
        re = near_sources[:, None, None, :, 0]
        im = near_sources[:, None, None, :, 1]
        turned = jnp.stack([re * cosines - im * sines, im * cosines + re * sines], axis=4)
        turned = turned.astype(jnp.bfloat16).reshape(mine * 2 * ROWS, total_windows * 2 * NB)
        lags = jnp.dot(turned, spectra, preferred_element_type=jnp.float32)
        lags = lags.reshape(mine, 2, ROWS, channels)
        sent = from_behind(lags[:, 1].astype(jnp.bfloat16), "chan", -key)
        pieces[key] = (lags[:, 0], sent)
    received, swapped = [], []
    for offset in range(OFFS):
        key = (offset - REACH) % blocks
        got = pair_list[(block_at - key) % blocks, offset].astype(jnp.float32)
        gave = pair_list[block_at, offset].astype(jnp.float32)
        received.append(pieces[key][0][:, :LAGS] * got)
        swapped.append(pieces[key][1][:, :LAGS].astype(jnp.float32) * gave)
    return jnp.stack(received, axis=1), jnp.stack(swapped, axis=1)


def solution(mesh):
    in_specs = (
        P(("groups", "win"), "chan", None),
        P(("groups", "chan")),
        P(),
        P("groups"),
        P("groups", None),
    )
    out_specs = (
        P(("win", "sub"), None, None, ("groups", "chan")),
        P(("groups", "chan", "win", "sub"), None, None, None),
    )
    return jax.shard_map(
        on_device, mesh=mesh, in_specs=in_specs, out_specs=out_specs, check_vma=False
    )
```

```python
import functools
import math

import jax
import jax.numpy as jnp
import numpy as np
from jax import lax
from jax.experimental import pallas as pl
from jax.experimental.pallas import tpu as pltpu
from jax.sharding import PartitionSpec as P

NB = 512
MAXLAG = 50
LAGS = 2 * MAXLAG + 1
SLOT = 104
STRIDE = 8
REACH = 2
VS = 8
OFFS = 5
FLOOR = 0.25
MESH = pl.DeviceIdType.MESH
FAR = (((1,), (1,)), ((), ()))


def dft_rows(samples):
    phases = np.arange(NB)[:, None] * np.arange(samples)[None, :] % samples
    angles = phases * (2.0 * math.pi / samples)
    return jnp.asarray(np.concatenate([np.cos(angles), -np.sin(angles)], axis=0), jnp.bfloat16)


def lag_rows(samples, factor):
    lags = np.zeros((SLOT,), np.int64)
    lags[:LAGS] = np.arange(LAGS) - MAXLAG
    angles = (lags[:, None] * np.arange(NB) % samples) * (2.0 * math.pi / samples)
    tables = np.stack([np.cos(angles), np.sin(angles)]) * factor
    return jnp.asarray(tables, jnp.float32)


def chunks_of(channels):
    cuts = [(0, 128)]
    while sum(cuts[-1]) < channels:
        start = sum(cuts[-1])
        cuts.append((start, min(256, channels - start)))
    return cuts


def kernel(keys, wins, subs, mine, rows, cuts, *refs):
    phase_ref, traces, mask, widths, dft, lag = refs[:6]
    fwd, own_back, far_back = refs[6:9]
    count = len(cuts)
    spectra = refs[9 : 9 + count]
    staged = refs[9 + count : 9 + 2 * count]
    (weights, own_sources, sources, far_rows, near_rows,
     s_send, s_recv, x_send, x_recv, c_send, c_recv, z_send, z_recv) = refs[9 + 2 * count :]
    samples = traces.shape[1]
    blocks = lax.axis_size("chan")
    block_at = lax.axis_index("chan")
    win_at = lax.axis_index("win")
    sub_at = lax.axis_index("sub")
    sub_peer = {"sub": 1 - sub_at}

    def peer(key, d):
        return {"chan": lax.rem(block_at + key, blocks), "win": lax.rem(win_at + d, wins)}

    others = [(key, d) for key in keys for d in range(wins) if (key, d) != (0, 0)]
    barrier = pltpu.get_barrier_semaphore()
    for key, d in others:
        pl.semaphore_signal(barrier, inc=1, device_id=peer(key, d), device_id_type=MESH)
    pl.semaphore_signal(barrier, inc=1, device_id=sub_peer, device_id_type=MESH)

    width_row = widths[...].astype(jnp.float32)
    width_col = jnp.transpose(jnp.broadcast_to(width_row, (128, NB)))[:, :1]
    at = lax.broadcasted_iota(jnp.int32, (NB, NB), 0)
    to = lax.broadcasted_iota(jnp.int32, (NB, NB), 1)
    near = jnp.abs(at - to).astype(jnp.float32) <= width_col
    weights[...] = jnp.where(near, 1.0, 0.0).astype(jnp.bfloat16)
    bins = lax.broadcasted_iota(jnp.int32, (NB, 1), 0).astype(jnp.float32)
    inside = jnp.minimum(bins + width_col, NB - 1.0) - jnp.maximum(bins - width_col, 0.0) + 1.0
    share = 1.0 / inside

    def whiten(i):
        start, width = cuts[i]
        cut = traces[start : start + width, :]
        scale = mask[:, start : start + width].astype(jnp.float32) * samples ** (-0.5)
        re = lax.dot_general(dft[:NB, :], cut, FAR, preferred_element_type=jnp.float32) * scale
        im = lax.dot_general(dft[NB:, :], cut, FAR, preferred_element_type=jnp.float32) * scale
        amplitude = jnp.sqrt(re * re + im * im)
        high = amplitude.astype(jnp.bfloat16)
        low = (amplitude - high.astype(jnp.float32)).astype(jnp.bfloat16)
        total = jnp.dot(weights[...], high, preferred_element_type=jnp.float32)
        total = total + jnp.dot(weights[...], low, preferred_element_type=jnp.float32)
        gain = 1.0 / jnp.maximum(total * share, FLOOR)
        spectra[i][:NB, :] = (re * gain).astype(jnp.bfloat16)
        spectra[i][NB : 2 * NB, :] = (im * gain).astype(jnp.bfloat16)

    def x_copies(i):
        src = pl.ds(pl.multiple_of(sub_at * NB, NB), NB)
        copies = []
        for d in range(1, wins):
            dst = pl.ds(pl.multiple_of(d * 2 * NB + sub_at * NB, NB), NB)
            copies.append(pltpu.make_async_remote_copy(
                src_ref=spectra[i].at[src], dst_ref=spectra[i].at[dst],
                send_sem=x_send.at[i, d - 1], recv_sem=x_recv.at[i, d - 1],
                device_id={"win": lax.rem(win_at + d, wins)}, device_id_type=MESH))
        return copies

    def c_copies(i):
        copies = []
        for d in range(1, wins):
            part = pl.ds(pl.multiple_of(d * 2 * NB + sub_at * NB, NB), NB)
            copies.append(pltpu.make_async_remote_copy(
                src_ref=spectra[i].at[part], dst_ref=spectra[i].at[part],
                send_sem=c_send.at[i, d - 1], recv_sem=c_recv.at[i, d - 1],
                device_id=sub_peer, device_id_type=MESH))
        return copies

    def z_copies(i):
        start, width = cuts[i]
        copies = []
        for n, key in enumerate(keys[1:]):
            copies.append(pltpu.make_async_remote_copy(
                src_ref=staged[i].at[n], dst_ref=far_back.at[n, :, start : start + width],
                send_sem=z_send.at[i, n], recv_sem=z_recv.at[i, n],
                device_id={"chan": lax.rem(block_at + blocks - key, blocks)}, device_id_type=MESH))
        return copies

    whiten(0)
    phase = phase_ref[block_at]
    row_ids = lax.broadcasted_iota(jnp.int32, (16, cuts[0][1]), 0)
    lane_ids = lax.broadcasted_iota(jnp.int32, (16, cuts[0][1]), 1)
    chosen = (lane_ids == phase + STRIDE * row_ids) & (row_ids < VS)
    picker = jnp.where(chosen, 1.0, 0.0).astype(jnp.bfloat16)
    picked = lax.dot_general(
        picker, spectra[0][: 2 * NB, :], FAR, preferred_element_type=jnp.float32)
    for v in range(VS):
        own_sources[v // mine, v % mine : v % mine + 1, :] = picked[v : v + 1, :]
    sources[0, 0] = own_sources[win_at * subs + sub_at]
    pl.semaphore_wait(barrier, len(others) + 1)

    s_copies = []
    for key, d in others:
        n = keys.index(key)
        s_copies.append(pltpu.make_async_remote_copy(
            src_ref=own_sources.at[lax.rem(win_at + d, wins) * subs + sub_at],
            dst_ref=sources.at[n, d],
            send_sem=s_send.at[n, d], recv_sem=s_recv.at[n, d],
            device_id=peer(key, d), device_id_type=MESH))
    for copy in s_copies:
        copy.start()
    over_x, over_c, over_z = [x_copies(0)], [], []
    for copy in over_x[0]:
        copy.start()
    for i in range(1, count):
        whiten(i)
        over_x.append(x_copies(i))
        for copy in over_x[i]:
            copy.start()

    def forward(i):
        over_c.append(c_copies(i))
        for arrived, onward in zip(over_x[i], over_c[i]):
            arrived.wait_recv()
            onward.start()

    forward(0)
    for copy in s_copies:
        copy.wait_recv()
    blank = rows - mine * SLOT

    def fill(target, at_row, sign, n, d):
        re_parts, im_parts = [], []
        for v in range(mine):
            re = sources[n, d, v : v + 1, :NB]
            im = sources[n, d, v : v + 1, NB:]
            cosines, sines = lag[0], lag[1] * sign
            re_parts.append(re * cosines - im * sines)
            im_parts.append(im * cosines + re * sines)
        if blank:
            re_parts.append(jnp.zeros((blank, NB), jnp.float32))
            im_parts.append(jnp.zeros((blank, NB), jnp.float32))
        base = d * 2 * NB
        span = slice(at_row, at_row + rows)
        target[span, base : base + NB] = jnp.concatenate(re_parts, axis=0).astype(jnp.bfloat16)
        target[span, base + NB : base + 2 * NB] = jnp.concatenate(im_parts, axis=0).astype(jnp.bfloat16)

    for n in range(1, len(keys)):
        for d in range(wins):
            fill(far_rows, (n - 1) * rows, -1.0, n, d)

    def send(i):
        for copy in over_c[i]:
            copy.wait_recv()
        lags = jnp.dot(far_rows[...], spectra[i][...], preferred_element_type=jnp.float32)
        for n in range(len(keys) - 1):
            staged[i][n] = lags[n * rows : (n + 1) * rows].astype(jnp.bfloat16)
        over_z.append(z_copies(i))
        for copy in over_z[i]:
            copy.start()

    def keep(i):
        start, width = cuts[i]
        lags = jnp.dot(near_rows[...], spectra[i][...], preferred_element_type=jnp.float32)
        for n in range(len(keys)):
            fwd[n, :, start : start + width] = lags[n * rows : (n + 1) * rows].astype(jnp.bfloat16)
        own_back[:, start : start + width] = lags[len(keys) * rows :].astype(jnp.bfloat16)

    send(0)
    for i in range(1, count):
        forward(i)
        if i == 1:
            for d in range(wins):
                for n in range(len(keys)):
                    fill(near_rows, n * rows, 1.0, n, d)
                fill(near_rows, len(keys) * rows, -1.0, 0, d)
        send(i)
    for i in range(count):
        keep(i)
    for copies in over_z:
        for copy in copies:
            copy.wait()
    for copies in over_x + over_c + [s_copies]:
        for copy in copies:
            copy.wait_send()


def on_device(traces, channel_mask, smooth_width, source_phase, pair_list):
    windows, channels, samples = traces.shape
    subs = lax.axis_size("sub")
    wins = lax.axis_size("win")
    blocks = lax.axis_size("chan")
    block_at = lax.axis_index("chan")
    mine = VS // (wins * subs)
    rows = -(-mine * SLOT // 16) * 16
    keys = [0]
    for offset in range(OFFS):
        key = (offset - REACH) % blocks
        if key not in keys:
            keys.append(key)
    nk = len(keys)
    depth = wins * 2 * NB
    cuts = chunks_of(channels)
    count = len(cuts)
    vmem = pl.BlockSpec(memory_space=pltpu.VMEM)
    dma = pltpu.SemaphoreType.DMA
    fwd, own_back, far_back = pl.pallas_call(
        functools.partial(kernel, keys, wins, subs, mine, rows, cuts),
        out_shape=[
            jax.ShapeDtypeStruct((nk, rows, channels), jnp.bfloat16),
            jax.ShapeDtypeStruct((rows, channels), jnp.bfloat16),
            jax.ShapeDtypeStruct((nk - 1, rows, channels), jnp.bfloat16),
        ],
        in_specs=[pl.BlockSpec(memory_space=pltpu.SMEM)] + [vmem] * 5,
        out_specs=[vmem, vmem, pl.BlockSpec(memory_space=pl.ANY)],
        scratch_shapes=[pltpu.VMEM((depth, width), jnp.bfloat16) for _, width in cuts]
        + [pltpu.VMEM((nk - 1, rows, width), jnp.bfloat16) for _, width in cuts]
        + [
            pltpu.VMEM((NB, NB), jnp.bfloat16),
            pltpu.VMEM((wins * subs, mine, 2 * NB), jnp.float32),
            pltpu.VMEM((nk, wins, mine, 2 * NB), jnp.float32),
            pltpu.VMEM(((nk - 1) * rows, depth), jnp.bfloat16),
            pltpu.VMEM(((nk + 1) * rows, depth), jnp.bfloat16),
            dma((nk, wins)), dma((nk, wins)),
            dma((count, wins - 1)), dma((count, wins - 1)),
            dma((count, wins - 1)), dma((count, wins - 1)),
            dma((count, nk - 1)), dma((count, nk - 1)),
        ],
        compiler_params=pltpu.CompilerParams(
            collective_id=0, has_side_effects=True, vmem_limit_bytes=56 * 2**20
        ),
        name="stacks",
    )(
        source_phase,
        traces.reshape(channels, samples),
        channel_mask.reshape(1, channels),
        smooth_width.reshape(1, NB),
        dft_rows(samples),
        lag_rows(samples, (NB * windows * wins) ** (-0.5)),
    )
    received, swapped = [], []
    for offset in range(OFFS):
        key = (offset - REACH) % blocks
        n = keys.index(key)
        got = pair_list[(block_at - key) % blocks, offset].astype(jnp.float32)
        gave = pair_list[block_at, offset].astype(jnp.float32)
        back = own_back if n == 0 else far_back[n - 1]
        for stack, cells, paired in ((received, fwd[n], got), (swapped, back, gave)):
            cells = cells[: mine * SLOT].reshape(mine, SLOT, channels)[:, :LAGS]
            stack.append(cells.astype(jnp.float32) * paired)
    return jnp.stack(received, axis=1), jnp.stack(swapped, axis=1)


def solution(mesh):
    in_specs = (
        P(("groups", "win"), "chan", None),
        P(("groups", "chan")),
        P(),
        P("groups"),
        P("groups", None),
    )
    out_specs = (
        P(("win", "sub"), None, None, ("groups", "chan")),
        P(("groups", "chan", "win", "sub"), None, None, None),
    )
    return jax.shard_map(
        on_device, mesh=mesh, in_specs=in_specs, out_specs=out_specs, check_vma=False
    )
```

```python
import functools
import math

import jax
import jax.numpy as jnp
import numpy as np
from jax import lax
from jax.experimental import pallas as pl
from jax.experimental.pallas import tpu as pltpu
from jax.sharding import PartitionSpec as P

NB = 512
MAXLAG = 50
LAGS = 2 * MAXLAG + 1
SLOT = 104
STRIDE = 8
REACH = 2
VS = 8
OFFS = 5
FLOOR = 0.25
MESH = pl.DeviceIdType.MESH
FAR = (((1,), (1,)), ((), ()))


def dft_rows(samples):
    phases = np.arange(NB)[:, None] * np.arange(samples)[None, :] % samples
    angles = phases * (2.0 * math.pi / samples)
    return jnp.asarray(np.concatenate([np.cos(angles), -np.sin(angles)], axis=0), jnp.bfloat16)


def lag_rows(samples, factor):
    lags = np.zeros((SLOT,), np.int64)
    lags[:LAGS] = np.arange(LAGS) - MAXLAG
    angles = (lags[:, None] * np.arange(NB) % samples) * (2.0 * math.pi / samples)
    tables = np.stack([np.cos(angles), np.sin(angles)]) * factor
    return jnp.asarray(tables, jnp.float32)


def chunks_of(channels):
    cuts = [(0, 128)]
    while sum(cuts[-1]) < channels:
        start = sum(cuts[-1])
        cuts.append((start, min(256, channels - start)))
    return cuts


def kernel(keys, wins, subs, mine, rows, cuts, *refs):
    phase_ref, pairs, traces, mask, widths, dft, lag = refs[:7]
    fwd, back = refs[7:9]
    count = len(cuts)
    spectra = refs[9 : 9 + count]
    staged = refs[9 + count : 9 + 2 * count]
    (far_back, weights, own_sources, sources, far_rows, near_rows,
     s_send, s_recv, x_send, x_recv, c_send, c_recv, z_send, z_recv) = refs[9 + 2 * count :]
    samples = traces.shape[1]
    blocks = lax.axis_size("chan")
    block_at = lax.axis_index("chan")
    win_at = lax.axis_index("win")
    sub_at = lax.axis_index("sub")
    sub_peer = {"sub": 1 - sub_at}

    def peer(key, d):
        return {"chan": lax.rem(block_at + key, blocks), "win": lax.rem(win_at + d, wins)}

    others = [(key, d) for key in keys for d in range(wins) if (key, d) != (0, 0)]
    barrier = pltpu.get_barrier_semaphore()
    for key, d in others:
        pl.semaphore_signal(barrier, inc=1, device_id=peer(key, d), device_id_type=MESH)
    pl.semaphore_signal(barrier, inc=1, device_id=sub_peer, device_id_type=MESH)

    width_row = widths[...].astype(jnp.float32)
    width_col = jnp.transpose(jnp.broadcast_to(width_row, (128, NB)))[:, :1]
    at = lax.broadcasted_iota(jnp.int32, (NB, NB), 0)
    to = lax.broadcasted_iota(jnp.int32, (NB, NB), 1)
    near = jnp.abs(at - to).astype(jnp.float32) <= width_col
    weights[...] = jnp.where(near, 1.0, 0.0).astype(jnp.bfloat16)
    bins = lax.broadcasted_iota(jnp.int32, (NB, 1), 0).astype(jnp.float32)
    inside = jnp.minimum(bins + width_col, NB - 1.0) - jnp.maximum(bins - width_col, 0.0) + 1.0
    share = 1.0 / inside

    def whiten(i):
        start, width = cuts[i]
        cut = traces[start : start + width, :]
        scale = mask[:, start : start + width].astype(jnp.float32) * samples ** (-0.5)
        re = lax.dot_general(dft[:NB, :], cut, FAR, preferred_element_type=jnp.float32) * scale
        im = lax.dot_general(dft[NB:, :], cut, FAR, preferred_element_type=jnp.float32) * scale
        amplitude = jnp.sqrt(re * re + im * im)
        high = amplitude.astype(jnp.bfloat16)
        low = (amplitude - high.astype(jnp.float32)).astype(jnp.bfloat16)
        total = jnp.dot(weights[...], high, preferred_element_type=jnp.float32)
        total = total + jnp.dot(weights[...], low, preferred_element_type=jnp.float32)
        gain = 1.0 / jnp.maximum(total * share, FLOOR)
        spectra[i][:NB, :] = (re * gain).astype(jnp.bfloat16)
        spectra[i][NB : 2 * NB, :] = (im * gain).astype(jnp.bfloat16)

    def x_copies(i):
        src = pl.ds(pl.multiple_of(sub_at * NB, NB), NB)
        copies = []
        for d in range(1, wins):
            dst = pl.ds(pl.multiple_of(d * 2 * NB + sub_at * NB, NB), NB)
            copies.append(pltpu.make_async_remote_copy(
                src_ref=spectra[i].at[src], dst_ref=spectra[i].at[dst],
                send_sem=x_send.at[i, d - 1], recv_sem=x_recv.at[i, d - 1],
                device_id={"win": lax.rem(win_at + d, wins)}, device_id_type=MESH))
        return copies

    def c_copies(i):
        copies = []
        for d in range(1, wins):
            part = pl.ds(pl.multiple_of(d * 2 * NB + sub_at * NB, NB), NB)
            copies.append(pltpu.make_async_remote_copy(
                src_ref=spectra[i].at[part], dst_ref=spectra[i].at[part],
                send_sem=c_send.at[i, d - 1], recv_sem=c_recv.at[i, d - 1],
                device_id=sub_peer, device_id_type=MESH))
        return copies

    def z_copies(i):
        start, width = cuts[i]
        copies = []
        for n, key in enumerate(keys[1:]):
            copies.append(pltpu.make_async_remote_copy(
                src_ref=staged[i].at[n], dst_ref=far_back.at[n, :, start : start + width],
                send_sem=z_send.at[i, n], recv_sem=z_recv.at[i, n],
                device_id={"chan": lax.rem(block_at + blocks - key, blocks)}, device_id_type=MESH))
        return copies

    whiten(0)
    phase = phase_ref[block_at]
    row_ids = lax.broadcasted_iota(jnp.int32, (16, cuts[0][1]), 0)
    lane_ids = lax.broadcasted_iota(jnp.int32, (16, cuts[0][1]), 1)
    chosen = (lane_ids == phase + STRIDE * row_ids) & (row_ids < VS)
    picker = jnp.where(chosen, 1.0, 0.0).astype(jnp.bfloat16)
    picked = lax.dot_general(
        picker, spectra[0][: 2 * NB, :], FAR, preferred_element_type=jnp.float32)
    for v in range(VS):
        own_sources[v // mine, v % mine : v % mine + 1, :] = picked[v : v + 1, :]
    sources[0, 0] = own_sources[win_at * subs + sub_at]
    pl.semaphore_wait(barrier, len(others) + 1)

    s_copies = []
    for key, d in others:
        n = keys.index(key)
        s_copies.append(pltpu.make_async_remote_copy(
            src_ref=own_sources.at[lax.rem(win_at + d, wins) * subs + sub_at],
            dst_ref=sources.at[n, d],
            send_sem=s_send.at[n, d], recv_sem=s_recv.at[n, d],
            device_id=peer(key, d), device_id_type=MESH))
    for copy in s_copies:
        copy.start()
    over_x, over_c, over_z = [x_copies(0)], [], []
    for copy in over_x[0]:
        copy.start()
    def feed(i):
        whiten(i)
        over_x.append(x_copies(i))
        for copy in over_x[i]:
            copy.start()

    feed(1)

    def forward(i):
        over_c.append(c_copies(i))
        for arrived, onward in zip(over_x[i], over_c[i]):
            arrived.wait_recv()
            onward.start()

    forward(0)
    for copy in s_copies:
        copy.wait_recv()

    def fill(target, at_row, sign, n, d):
        cosines, sines = lag[0], lag[1] * sign
        re_parts, im_parts = [], []
        for v in range(mine):
            re = sources[n, d, v : v + 1, :NB]
            im = sources[n, d, v : v + 1, NB:]
            re_parts.append(re * cosines - im * sines)
            im_parts.append(im * cosines + re * sines)
        if rows > mine * SLOT:
            re_parts.append(jnp.zeros((rows - mine * SLOT, NB), jnp.float32))
            im_parts.append(jnp.zeros((rows - mine * SLOT, NB), jnp.float32))
        base = d * 2 * NB
        span = slice(at_row, at_row + rows)
        target[span, base : base + NB] = jnp.concatenate(re_parts, axis=0).astype(jnp.bfloat16)
        target[span, base + NB : base + 2 * NB] = jnp.concatenate(im_parts, axis=0).astype(jnp.bfloat16)

    for n in range(1, len(keys)):
        for d in range(wins):
            fill(far_rows, (n - 1) * rows, -1.0, n, d)

    def send(i):
        for copy in over_c[i]:
            copy.wait_recv()
        lags = jnp.dot(far_rows[...], spectra[i][...], preferred_element_type=jnp.float32)
        for n in range(len(keys) - 1):
            staged[i][n] = lags[n * rows : (n + 1) * rows].astype(jnp.bfloat16)
        over_z.append(z_copies(i))
        for copy in over_z[i]:
            copy.start()

    def keep(i):
        start, width = cuts[i]
        lags = jnp.dot(near_rows[...], spectra[i][...], preferred_element_type=jnp.float32)
        for offset in range(OFFS):
            n = keys.index((offset - REACH) % blocks)
            got = pairs[lax.rem(block_at + 2 * blocks - offset + REACH, blocks), offset].astype(jnp.float32)
            cells = lags[n * rows : (n + 1) * rows] * got
            fwd[offset, :, start : start + width] = cells.astype(jnp.bfloat16)
        gave = pairs[block_at, REACH].astype(jnp.float32)
        back[REACH, :, start : start + width] = (lags[len(keys) * rows :] * gave).astype(jnp.bfloat16)

    send(0)
    for i in range(1, count):
        if i + 1 < count:
            feed(i + 1)
        else:
            for d in range(wins):
                for n in range(len(keys)):
                    fill(near_rows, n * rows, 1.0, n, d)
                fill(near_rows, len(keys) * rows, -1.0, 0, d)
        forward(i)
        send(i)
    for i in range(count):
        keep(i)
    for i, (start, width) in enumerate(cuts):
        for copy in over_z[i]:
            copy.wait()
        for offset in range(OFFS):
            n = keys.index((offset - REACH) % blocks)
            if n:
                gave = pairs[block_at, offset].astype(jnp.bfloat16)
                back[offset, :, start : start + width] = far_back[n - 1, :, start : start + width] * gave
    for copies in over_x + over_c + [s_copies]:
        for copy in copies:
            copy.wait_send()


def on_device(traces, channel_mask, smooth_width, source_phase, pair_list):
    windows, channels, samples = traces.shape
    subs = lax.axis_size("sub")
    wins = lax.axis_size("win")
    blocks = lax.axis_size("chan")
    mine = VS // (wins * subs)
    rows = -(-mine * SLOT // 16) * 16
    keys = [0]
    for offset in range(OFFS):
        key = (offset - REACH) % blocks
        if key not in keys:
            keys.append(key)
    nk = len(keys)
    depth = wins * 2 * NB
    cuts = chunks_of(channels)
    count = len(cuts)
    vmem = pl.BlockSpec(memory_space=pltpu.VMEM)
    dma = pltpu.SemaphoreType.DMA
    smem = pl.BlockSpec(memory_space=pltpu.SMEM)
    stack = jax.ShapeDtypeStruct((OFFS, rows, channels), jnp.bfloat16)
    stacks = pl.pallas_call(
        functools.partial(kernel, keys, wins, subs, mine, rows, cuts),
        out_shape=[stack, stack],
        in_specs=[smem] * 2 + [vmem] * 5,
        out_specs=[vmem, vmem],
        scratch_shapes=[pltpu.VMEM((depth, width), jnp.bfloat16) for _, width in cuts]
        + [pltpu.VMEM((nk - 1, rows, width), jnp.bfloat16) for _, width in cuts]
        + [
            pltpu.VMEM((nk - 1, rows, channels), jnp.bfloat16),
            pltpu.VMEM((NB, NB), jnp.bfloat16),
            pltpu.VMEM((wins * subs, mine, 2 * NB), jnp.float32),
            pltpu.VMEM((nk, wins, mine, 2 * NB), jnp.float32),
            pltpu.VMEM(((nk - 1) * rows, depth), jnp.bfloat16),
            pltpu.VMEM(((nk + 1) * rows, depth), jnp.bfloat16),
            dma((nk, wins)), dma((nk, wins)),
            dma((count, wins - 1)), dma((count, wins - 1)),
            dma((count, wins - 1)), dma((count, wins - 1)),
            dma((count, nk - 1)), dma((count, nk - 1)),
        ],
        compiler_params=pltpu.CompilerParams(
            collective_id=0, has_side_effects=True, vmem_limit_bytes=56 * 2**20
        ),
        name="stacks",
    )(
        source_phase,
        pair_list,
        traces.reshape(channels, samples),
        channel_mask.reshape(1, channels),
        smooth_width.reshape(1, NB),
        dft_rows(samples),
        lag_rows(samples, (NB * windows * wins) ** (-0.5)),
    )
    outs = []
    for cells in stacks:
        cells = cells[:, : mine * SLOT].reshape(OFFS, mine, SLOT, channels)[:, :, :LAGS]
        outs.append(jnp.transpose(cells, (1, 0, 2, 3)).astype(jnp.float32))
    return tuple(outs)


def solution(mesh):
    in_specs = (
        P(("groups", "win"), "chan", None),
        P(("groups", "chan")),
        P(),
        P("groups"),
        P("groups", None),
    )
    out_specs = (
        P(("win", "sub"), None, None, ("groups", "chan")),
        P(("groups", "chan", "win", "sub"), None, None, None),
    )
    return jax.shard_map(
        on_device, mesh=mesh, in_specs=in_specs, out_specs=out_specs, check_vma=False
    )
```

```python
import functools
import math

import jax
import jax.numpy as jnp
import numpy as np
from jax import lax
from jax.experimental import pallas as pl
from jax.experimental.pallas import tpu as pltpu
from jax.sharding import PartitionSpec as P

NB = 512
MAXLAG = 50
LAGS = 2 * MAXLAG + 1
SLOT = 104
STRIDE = 8
REACH = 2
VS = 8
OFFS = 5
FLOOR = 0.25
MESH = pl.DeviceIdType.MESH
FAR = (((1,), (1,)), ((), ()))


def dft_rows(samples):
    phases = np.arange(NB)[:, None] * np.arange(samples)[None, :] % samples
    angles = phases * (2.0 * math.pi / samples)
    return jnp.asarray(np.concatenate([np.cos(angles), -np.sin(angles)], axis=0), jnp.bfloat16)


def lag_rows(samples, factor):
    lags = np.zeros((SLOT,), np.int64)
    lags[:LAGS] = np.arange(LAGS) - MAXLAG
    angles = (lags[:, None] * np.arange(NB) % samples) * (2.0 * math.pi / samples)
    tables = np.stack([np.cos(angles), np.sin(angles)]) * factor
    return jnp.asarray(tables, jnp.float32)


def chunks_of(channels):
    cuts = [(0, 128)]
    while sum(cuts[-1]) < channels:
        start = sum(cuts[-1])
        cuts.append((start, min(256, channels - start)))
    return cuts


def kernel(keys, wins, subs, mine, rows, cuts, *refs):
    phase_ref, pairs, traces, mask, widths, dft, lag = refs[:7]
    fwd, back = refs[7:9]
    count = len(cuts)
    spectra = refs[9 : 9 + count]
    staged = refs[9 + count : 9 + 2 * count]
    (far_back, weights, own_sources, sources, far_rows, near_rows,
     s_send, s_recv, x_send, x_recv, c_send, c_recv, z_send, z_recv) = refs[9 + 2 * count :]
    samples = traces.shape[1]
    blocks = lax.axis_size("chan")
    block_at = lax.axis_index("chan")
    win_at = lax.axis_index("win")
    sub_at = lax.axis_index("sub")
    sub_peer = {"sub": 1 - sub_at}

    def peer(key, d):
        return {"chan": lax.rem(block_at + key, blocks), "win": lax.rem(win_at + d, wins)}

    others = [(key, d) for key in keys for d in range(wins) if (key, d) != (0, 0)]
    barrier = pltpu.get_barrier_semaphore()
    for key, d in others:
        pl.semaphore_signal(barrier, inc=1, device_id=peer(key, d), device_id_type=MESH)
    pl.semaphore_signal(barrier, inc=1, device_id=sub_peer, device_id_type=MESH)

    width_row = widths[...].astype(jnp.float32)
    width_col = jnp.transpose(jnp.broadcast_to(width_row, (128, NB)))[:, :1]
    at = lax.broadcasted_iota(jnp.int32, (NB, NB), 0)
    to = lax.broadcasted_iota(jnp.int32, (NB, NB), 1)
    near = jnp.abs(at - to).astype(jnp.float32) <= width_col
    weights[...] = jnp.where(near, 1.0, 0.0).astype(jnp.bfloat16)
    bins = lax.broadcasted_iota(jnp.int32, (NB, 1), 0).astype(jnp.float32)
    inside = jnp.minimum(bins + width_col, NB - 1.0) - jnp.maximum(bins - width_col, 0.0) + 1.0
    share = 1.0 / inside

    def whiten(i):
        start, width = cuts[i]
        cut = traces[start : start + width, :]
        scale = mask[start : start + width].reshape(1, width).astype(jnp.float32) * samples ** (-0.5)
        re = lax.dot_general(dft[:NB, :], cut, FAR, preferred_element_type=jnp.float32) * scale
        im = lax.dot_general(dft[NB:, :], cut, FAR, preferred_element_type=jnp.float32) * scale
        amplitude = jnp.sqrt(re * re + im * im)
        high = amplitude.astype(jnp.bfloat16)
        low = (amplitude - high.astype(jnp.float32)).astype(jnp.bfloat16)
        total = jnp.dot(weights[...], high, preferred_element_type=jnp.float32)
        total = total + jnp.dot(weights[...], low, preferred_element_type=jnp.float32)
        gain = 1.0 / jnp.maximum(total * share, FLOOR)
        spectra[i][:NB, :] = (re * gain).astype(jnp.bfloat16)
        spectra[i][NB : 2 * NB, :] = (im * gain).astype(jnp.bfloat16)

    def x_copies(i):
        src = pl.ds(pl.multiple_of(sub_at * NB, NB), NB)
        copies = []
        for d in range(1, wins):
            dst = pl.ds(pl.multiple_of(d * 2 * NB + sub_at * NB, NB), NB)
            copies.append(pltpu.make_async_remote_copy(
                src_ref=spectra[i].at[src], dst_ref=spectra[i].at[dst],
                send_sem=x_send.at[i, d - 1], recv_sem=x_recv.at[i, d - 1],
                device_id={"win": lax.rem(win_at + d, wins)}, device_id_type=MESH))
        return copies

    def c_copies(i):
        copies = []
        for d in range(1, wins):
            part = pl.ds(pl.multiple_of(d * 2 * NB + sub_at * NB, NB), NB)
            copies.append(pltpu.make_async_remote_copy(
                src_ref=spectra[i].at[part], dst_ref=spectra[i].at[part],
                send_sem=c_send.at[i, d - 1], recv_sem=c_recv.at[i, d - 1],
                device_id=sub_peer, device_id_type=MESH))
        return copies

    def z_copies(i):
        start, width = cuts[i]
        copies = []
        for n, key in enumerate(keys[1:]):
            copies.append(pltpu.make_async_remote_copy(
                src_ref=staged[i].at[n], dst_ref=far_back.at[n, :, start : start + width],
                send_sem=z_send.at[i, n], recv_sem=z_recv.at[i, n],
                device_id={"chan": lax.rem(block_at + blocks - key, blocks)}, device_id_type=MESH))
        return copies

    whiten(0)
    phase = phase_ref[block_at]
    row_ids = lax.broadcasted_iota(jnp.int32, (16, cuts[0][1]), 0)
    lane_ids = lax.broadcasted_iota(jnp.int32, (16, cuts[0][1]), 1)
    chosen = (lane_ids == phase + STRIDE * row_ids) & (row_ids < VS)
    picker = jnp.where(chosen, 1.0, 0.0).astype(jnp.bfloat16)
    picked = lax.dot_general(
        picker, spectra[0][: 2 * NB, :], FAR, preferred_element_type=jnp.float32)
    for v in range(VS):
        own_sources[v // mine, v % mine : v % mine + 1, :] = picked[v : v + 1, :]
    sources[0, 0] = own_sources[win_at * subs + sub_at]
    pl.semaphore_wait(barrier, len(others) + 1)

    s_copies = []
    for key, d in others:
        n = keys.index(key)
        s_copies.append(pltpu.make_async_remote_copy(
            src_ref=own_sources.at[lax.rem(win_at + d, wins) * subs + sub_at],
            dst_ref=sources.at[n, d],
            send_sem=s_send.at[n, d], recv_sem=s_recv.at[n, d],
            device_id=peer(key, d), device_id_type=MESH))
    for copy in s_copies:
        copy.start()
    over_x, over_c, over_z = [x_copies(0)], [], []
    for copy in over_x[0]:
        copy.start()
    def feed(i):
        whiten(i)
        over_x.append(x_copies(i))
        for copy in over_x[i]:
            copy.start()

    feed(1)

    def forward(i):
        over_c.append(c_copies(i))
        for arrived, onward in zip(over_x[i], over_c[i]):
            arrived.wait_recv()
            onward.start()

    forward(0)
    for copy in s_copies:
        copy.wait_recv()

    def fill(target, at_row, sign, n, d):
        cosines, sines = lag[0], lag[1] * sign
        re_parts, im_parts = [], []
        for v in range(mine):
            re = sources[n, d, v : v + 1, :NB]
            im = sources[n, d, v : v + 1, NB:]
            re_parts.append(re * cosines - im * sines)
            im_parts.append(im * cosines + re * sines)
        if rows > mine * SLOT:
            re_parts.append(jnp.zeros((rows - mine * SLOT, NB), jnp.float32))
            im_parts.append(jnp.zeros((rows - mine * SLOT, NB), jnp.float32))
        base = d * 2 * NB
        span = slice(at_row, at_row + rows)
        target[span, base : base + NB] = jnp.concatenate(re_parts, axis=0).astype(jnp.bfloat16)
        target[span, base + NB : base + 2 * NB] = jnp.concatenate(im_parts, axis=0).astype(jnp.bfloat16)

    for n in range(1, len(keys)):
        for d in range(wins):
            fill(far_rows, (n - 1) * rows, -1.0, n, d)

    def send(i):
        for copy in over_c[i]:
            copy.wait_recv()
        lags = jnp.dot(far_rows[...], spectra[i][...], preferred_element_type=jnp.float32)
        for n in range(len(keys) - 1):
            staged[i][n] = lags[n * rows : (n + 1) * rows].astype(jnp.bfloat16)
        over_z.append(z_copies(i))
        for copy in over_z[i]:
            copy.start()

    def keep(i):
        start, width = cuts[i]
        lags = jnp.dot(near_rows[...], spectra[i][...], preferred_element_type=jnp.float32)
        for offset in range(OFFS):
            n = keys.index((offset - REACH) % blocks)
            got = pairs[lax.rem(block_at + 2 * blocks - offset + REACH, blocks), offset].astype(jnp.float32)
            cells = lags[n * rows : (n + 1) * rows] * got
            fwd[offset, :, start : start + width] = cells.astype(jnp.bfloat16)
        gave = pairs[block_at, REACH].astype(jnp.float32)
        back[REACH, :, start : start + width] = (lags[len(keys) * rows :] * gave).astype(jnp.bfloat16)

    send(0)
    for i in range(1, count):
        if i + 1 < count:
            feed(i + 1)
        else:
            for d in range(wins):
                for n in range(len(keys)):
                    fill(near_rows, n * rows, 1.0, n, d)
                fill(near_rows, len(keys) * rows, -1.0, 0, d)
        forward(i)
        send(i)
    for i in range(count):
        keep(i)
    for i, (start, width) in enumerate(cuts):
        for copy in over_z[i]:
            copy.wait()
        for offset in range(OFFS):
            n = keys.index((offset - REACH) % blocks)
            if n:
                gave = pairs[block_at, offset].astype(jnp.bfloat16)
                back[offset, :, start : start + width] = far_back[n - 1, :, start : start + width] * gave
    for copies in over_x + over_c + [s_copies]:
        for copy in copies:
            copy.wait_send()


def on_device(traces, channel_mask, smooth_width, source_phase, pair_list):
    windows, channels, samples = traces.shape
    subs = lax.axis_size("sub")
    wins = lax.axis_size("win")
    blocks = lax.axis_size("chan")
    mine = VS // (wins * subs)
    rows = -(-mine * SLOT // 16) * 16
    keys = [0]
    for offset in range(OFFS):
        key = (offset - REACH) % blocks
        if key not in keys:
            keys.append(key)
    nk = len(keys)
    depth = wins * 2 * NB
    cuts = chunks_of(channels)
    count = len(cuts)
    vmem = pl.BlockSpec(memory_space=pltpu.VMEM)
    dma = pltpu.SemaphoreType.DMA
    smem = pl.BlockSpec(memory_space=pltpu.SMEM)
    stack = jax.ShapeDtypeStruct((OFFS, rows, channels), jnp.bfloat16)
    stacks = pl.pallas_call(
        functools.partial(kernel, keys, wins, subs, mine, rows, cuts),
        out_shape=[stack, stack],
        in_specs=[smem] * 2 + [vmem] * 5,
        out_specs=[vmem, vmem],
        scratch_shapes=[pltpu.VMEM((depth, width), jnp.bfloat16) for _, width in cuts]
        + [pltpu.VMEM((nk - 1, rows, width), jnp.bfloat16) for _, width in cuts]
        + [
            pltpu.VMEM((nk - 1, rows, channels), jnp.bfloat16),
            pltpu.VMEM((NB, NB), jnp.bfloat16),
            pltpu.VMEM((wins * subs, mine, 2 * NB), jnp.float32),
            pltpu.VMEM((nk, wins, mine, 2 * NB), jnp.float32),
            pltpu.VMEM(((nk - 1) * rows, depth), jnp.bfloat16),
            pltpu.VMEM(((nk + 1) * rows, depth), jnp.bfloat16),
            dma((nk, wins)), dma((nk, wins)),
            dma((count, wins - 1)), dma((count, wins - 1)),
            dma((count, wins - 1)), dma((count, wins - 1)),
            dma((count, nk - 1)), dma((count, nk - 1)),
        ],
        compiler_params=pltpu.CompilerParams(
            collective_id=0, has_side_effects=True, vmem_limit_bytes=56 * 2**20
        ),
        name="stacks",
    )(
        source_phase,
        pair_list,
        traces.reshape(channels, samples),
        channel_mask,
        smooth_width.reshape(1, NB),
        dft_rows(samples),
        lag_rows(samples, (NB * windows * wins) ** (-0.5)),
    )
    outs = []
    for cells in stacks:
        cells = cells[:, : mine * SLOT].reshape(OFFS, mine, SLOT, channels)[:, :, :LAGS]
        outs.append(jnp.transpose(cells, (1, 0, 2, 3)).astype(jnp.float32))
    return tuple(outs)


def solution(mesh):
    in_specs = (
        P(("groups", "win"), "chan", None),
        P(("groups", "chan")),
        P(),
        P("groups"),
        P("groups", None),
    )
    out_specs = (
        P(("win", "sub"), None, None, ("groups", "chan")),
        P(("groups", "chan", "win", "sub"), None, None, None),
    )
    return jax.shard_map(
        on_device, mesh=mesh, in_specs=in_specs, out_specs=out_specs, check_vma=False
    )
```
